32 devices in a mesh: dp: 4 (over x, core), expert: 8 (over z, y).
Axes of the slice: x: 2, y: 2, z: 4, core: 2. Of those that a mesh axis runs over, the one named last changes fastest.
Arguments:
- tokens: bfloat16 [6144, 1024], P(('dp', 'expert')), may hold values from -6 to 6
- route_ids: int32 [6144, 4], P(('dp', 'expert')), may hold values from 0 to 7, all different within a row; in each aligned block of 192 rows (0 to 191, 192 to 383, ...) at most 144 rows name the same one
- gate_weight: float32 [6144, 4], P(('dp', 'expert')), may hold values from 0.25 to 1
- old_owner: int32 [8], replicated, may hold values from 0 to 7, as said below
- new_owner: int32 [8], replicated, may hold values from 0 to 7, as said below
- weights: bfloat16 [8, 3, 1024, 1024], P('expert', None, None, 'dp'), may hold values from -0.1875 to 0.1875
- first_moment: float32 [8, 3, 1024, 1024], P('expert', None, None, 'dp'), may hold values from -6 to 6
- second_moment: float32 [8, 3, 1024, 1024], P('expert', None, None, 'dp'), may hold values from 0.01 to 4
Outputs:
- layer_output: bfloat16 [6144, 1024], P(('dp', 'expert'))
- new_weights: bfloat16 [8, 3, 1024, 1024], P('expert', None, None, 'dp')
- new_first_moment: float32 [8, 3, 1024, 1024], P('expert', None, None, 'dp')
- new_second_moment: float32 [8, 3, 1024, 1024], P('expert', None, None, 'dp')
The draws below stay inside these ranges and needn't reach their ends.
Inputs may be any that keep to these rules, and one draw needn't show every extreme that they name: `old_owner`: A permutation of the slots. `new_owner`: A permutation of the slots that differs from old_owner in exactly 2 experts. `route_ids`: the 4 experts of a row differ. In the 192 rows of one device no expert is named more than 144 times, a bound that some block reaches.
All inputs are finite; a program needn't handle non-finite values.
Results may differ from the reference program's by a relative error of at most 0.0058.
Values may be sent and summed in bfloat16 or wider, within the bound.
No kernel may reach another device: no remote copies, remote signals or barrier semaphores. Data moves between devices by JAX's collectives and lax.ppermute only.
A program may use at most 128 MiB of HBM per device.

```python
import math
import jax
import jax.numpy as jnp
import numpy as np
from jax import lax

D = 1024
H = 1024
TOP = 4
TOK_DEV = 192
EXPERTS = 8
CAP = 144
MOVES = 2
TOKENS = 6144
N_DP = 4
N_EXPERT = 8


def owner_plan(key):
    base = jax.random.fold_in(key, 7)
    first_key, second_key = jax.random.split(base)
    before = jax.random.permutation(first_key, EXPERTS).astype(jnp.int32)
    moving = jax.random.permutation(second_key, EXPERTS)[:MOVES].astype(jnp.int32)
    after = before.at[moving].set(before[jnp.roll(moving, 1)])
    return (before, after)


def draw_old_owner(key, part):
    return owner_plan(key)[0]


def draw_new_owner(key, part):
    return owner_plan(key)[1]


def shard_levels(stream_key, dims, cuts, least, high):
    factor_of = 1.0
    for dim, shards_of in cuts:
        draws = jax.random.uniform(jax.random.fold_in(jax.random.fold_in(stream_key, 6), dim), (shards_of,), jnp.float32, least / len(cuts), high / len(cuts))
        factor_of = factor_of * jnp.repeat(jnp.exp(draws), dims[dim] // shards_of).reshape((-1,) + (1,) * (len(dims) - 1 - dim))
    return factor_of


def assign_block(stream_key, own, number, rows, number_of, top, bound, slope):
    ranking = jax.random.permutation(stream_key, number_of)
    crowded, usual = shares(number_of, rows * top, bound, slope, True), shares(number_of, rows * top, bound, slope, False)
    places = jnp.arange(number_of)

    def named(lengths, offset_by):
        used = int((lengths > 0).sum())
        fixed = max(1, used // 4)
        moved = fixed + (places - fixed + offset_by * (used - fixed)) % max(1, number_of - fixed)
        return jnp.zeros((number_of,), jnp.int32).at[ranking[jnp.where(places < fixed, places, moved)]].set(jnp.asarray(lengths, jnp.int32))

    lengths = jnp.where(number % 4 == 0, named(crowded, number // 4), named(usual, number - number // 4 - 1))
    mixed = jax.random.permutation(jax.random.fold_in(own, 3), number_of)
    giver, taker = mixed[0:number_of // 2 * 2:2], mixed[1:number_of // 2 * 2:2]
    room = jnp.minimum(lengths[giver] - 1, bound - lengths[taker]) // 2
    room = jnp.where((giver == ranking[0]) | (taker == ranking[0]) | (lengths[taker] == 0), 0, jnp.maximum(room, 0))
    moved = jax.random.randint(jax.random.fold_in(own, 4), (number_of // 2,), 0, 1 << 20) % (room + 1)
    lengths = lengths.at[giver].add(-moved).at[taker].add(moved)
    items = jnp.searchsorted(jnp.cumsum(lengths), jnp.arange(rows * top), side="right").astype(jnp.int32)
    table = items.reshape(top, rows).T
    table = table[jax.random.permutation(jax.random.fold_in(own, 1), rows)]
    offset_by = jax.random.randint(jax.random.fold_in(own, 2), (rows, 1), 0, top)
    return jnp.take_along_axis(table, (jnp.arange(top)[None, :] + offset_by) % top, axis=1)


def shares(count, total, bound, slope, full):
    portions = [(1 << 20) // math.isqrt(grade ** slope) + 1 for grade in range(1, count + 1)]
    largest = bound if full else min(bound, max(-(-total // count), total * portions[0] // sum(portions)))
    least = 1 if total - largest >= count - 1 else 0
    holding, surplus = [largest] + [least] * (count - 1), total - largest - least * (count - 1)
    while surplus > 0:
        free = [i for i in range(1, count) if holding[i] < largest] or [i for i in range(1, count) if holding[i] < bound]
        whole, remaining = sum([portions[i] for i in free]), surplus
        for i in free:
            more = min(bound - holding[i], max(1, remaining * portions[i] // whole), surplus)
            holding[i] = holding[i] + more
            surplus = surplus - more
    return np.array(holding)


def noise(rng, extent, deviation, bound, shards=(), held_as=jnp.bfloat16):
    loudness = shard_levels(rng, extent, shards, -0.22, 0.18) if shards else 1.0
    entries = jax.random.normal(rng, extent, jnp.float32) * deviation * loudness
    return jnp.minimum(jnp.maximum(entries, -bound), bound).astype(held_as)


def setup_inputs(seed: int = 0) -> dict:
    splits = jax.random.split(jax.random.key(seed), 9)
    tokens = noise(splits[0], (TOKENS, D), 1.0, 6.0, ((0, 32),))
    route_ids_keys = jax.random.split(jax.random.fold_in(splits[1], 1), TOKENS // TOK_DEV)
    route_ids_turns = jax.random.permutation(jax.random.fold_in(splits[1], 3), TOKENS // TOK_DEV)
    route_ids = jax.vmap(lambda own, number: assign_block(jax.random.fold_in(splits[1], 2), own, number, TOK_DEV, EXPERTS, TOP, CAP, 2))(route_ids_keys, route_ids_turns).reshape((TOKENS, TOP))
    gate_weight = jnp.clip(0.25 + 0.75 * jax.random.uniform(splits[2], (TOKENS, TOP), jnp.float32) ** shard_levels(splits[2], (TOKENS, TOP), ((0, 32),), -0.2, 0.2), 0.25, 1.0)
    old_owner = draw_old_owner(jax.random.fold_in(splits[8], 71), 0)
    new_owner = draw_new_owner(jax.random.fold_in(splits[8], 71), 0)
    weights = noise(splits[5], (EXPERTS, 3, D, H), D ** -0.5, 0.1875, ((0, 8), (3, 4)))
    first_moment = noise(splits[6], (EXPERTS, 3, D, H), 1.0, 6.0, ((0, 8), (3, 4)), jnp.float32)
    second_moment = jnp.clip(jnp.exp(math.log(4.0) - 5.9914646 * jax.random.uniform(splits[7], (EXPERTS, 3, D, H), jnp.float32) ** shard_levels(splits[7], (EXPERTS, 3, D, H), ((0, 8), (3, 4)), -0.2, 0.2)), 0.01, 4.0)
    return {"tokens": tokens, "route_ids": route_ids, "gate_weight": gate_weight, "old_owner": old_owner, "new_owner": new_owner, "weights": weights, "first_moment": first_moment, "second_moment": second_moment}


def reference(tokens, route_ids, gate_weight, old_owner, new_owner, weights, first_moment, second_moment):
    source_slot = jnp.zeros((EXPERTS,), jnp.int32).at[new_owner].set(old_owner)
    new_weights = jnp.take(weights, source_slot, axis=0)
    new_first = jnp.take(first_moment, source_slot, axis=0)
    new_second = jnp.take(second_moment, source_slot, axis=0)
    expert_ids = route_ids.reshape(-1)
    count_all = expert_ids.shape[0]
    labels = jnp.arange(EXPERTS, dtype=jnp.int32)
    matches = (expert_ids[:, None] == labels[None, :]).astype(jnp.int32)
    position = jnp.sum((jnp.cumsum(matches, axis=0) - 1) * matches, axis=1).astype(jnp.int32)
    limit = CAP * N_DP * N_EXPERT
    token_index = (jnp.arange(count_all, dtype=jnp.int32) // TOP).astype(jnp.int32)
    table = jnp.zeros((EXPERTS, limit), jnp.int32).at[expert_ids, position].set(token_index)
    by_expert = jnp.take(weights, old_owner, axis=0)

    def run_expert(item):
        row_index, matrices = item
        chosen = jnp.take(tokens, row_index, axis=0)
        gate_part = jnp.dot(chosen, matrices[0], preferred_element_type=jnp.float32)
        up_part = jnp.dot(chosen, matrices[1], preferred_element_type=jnp.float32)
        hidden = (jax.nn.silu(gate_part) * up_part).astype(jnp.bfloat16)
        return jnp.dot(hidden, matrices[2].T, preferred_element_type=jnp.float32).astype(jnp.bfloat16)

    results = lax.map(run_expert, (table, by_expert))
    picked = results[expert_ids, position].astype(jnp.float32).reshape(TOKENS, TOP, D)
    layer_output = jnp.sum(picked * gate_weight[:, :, None], axis=1).astype(jnp.bfloat16)
    return (layer_output, new_weights, new_first, new_second)
```

```python
import functools
import itertools

import jax
import jax.numpy as jnp
from jax import lax
from jax.experimental import pallas as pl
from jax.experimental.pallas import tpu as pltpu
from jax.sharding import PartitionSpec as P

LANES = 128
PAIR_LIMIT = 64


def ring_pairs(count):
    order = list(range(0, count, 2)) + list(range(1, count, 2))[::-1]
    ahead = [(order[i], order[(i + 1) % count]) for i in range(count)]
    return ahead, [(b, a) for a, b in ahead]


def relay_of(source, target, count):
    if source ^ 1 != target:
        return source ^ 1
    beyond = target + 2
    return beyond if beyond < count else target - 2


def swap_slots(pair, dp_count, count, payload):
    low, high = pair
    low_relay, high_relay = relay_of(low, high, count), relay_of(high, low, count)

    def spread(core, edges):
        return [
            (row * count + a, row * count + b) for row in range(core, dp_count, 2) for a, b in edges
        ]

    direct = spread(0, [(low, high), (high, low)])
    first_hop = spread(1, [(low, low_relay), (high, high_relay)])
    second_hop = spread(1, [(low_relay, high), (high_relay, low)])
    axes = ("dp", "expert")
    first = [lax.ppermute(block, axes, direct + first_hop) for block in payload]
    return tuple((block, lax.ppermute(block, axes, second_hop)) for block in first)


def any_permutation(source_slot, payload):
    count = lax.axis_size("expert")
    moved = []
    for block in payload:
        rows = block.reshape(count, -1, block.shape[3])
        spread = lax.all_to_all(rows, "expert", split_axis=0, concat_axis=0, tiled=True)
        ordered = jnp.take(spread, source_slot, axis=0)
        back = lax.all_to_all(ordered, "expert", split_axis=0, concat_axis=0, tiled=True)
        back = back.reshape(block.shape)
        moved.append((back, back))
    return tuple(moved)


def relocate(arrays, old_owner, new_owner, source_slot, dp_count, count):
    payload = tuple(a.astype(jnp.bfloat16) for a in arrays)
    pairs = list(itertools.combinations(range(count), 2))
    if len(pairs) > PAIR_LIMIT:
        moved = any_permutation(source_slot, payload)
    else:
        differs = old_owner != new_owner
        low = jnp.min(jnp.where(differs, old_owner, count))
        high = jnp.max(jnp.where(differs, old_owner, 0))
        number = low * count - low * (low + 1) // 2 + high - low - 1
        branch = jnp.where(jnp.sum(differs.astype(jnp.int32)) == 2, number, len(pairs))
        branches = [
            functools.partial(lambda pair, *p: swap_slots(pair, dp_count, count, p), pair)
            for pair in pairs
        ] + [lambda *p: any_permutation(source_slot, p)]
        moved = lax.switch(branch, branches, *payload)
    slot = lax.axis_index("expert")
    here = jnp.sum(jnp.where(jnp.arange(count) == slot, source_slot, 0)) != slot
    odd = lax.axis_index("dp") % 2 == 1
    return tuple(
        jnp.where(here, jnp.where(odd, relayed, direct).astype(own.dtype), own)
        for own, (direct, relayed) in zip(arrays, moved)
    )


def expert_kernel(blocks, shards, width, count, slot_ref, *refs):
    rows_refs, weight_refs, out_refs = (
        refs[:blocks],
        refs[blocks : blocks + shards],
        refs[blocks + shards :],
    )
    rows = jnp.concatenate([r[:, :width] for r in rows_refs], axis=0)
    extra = jnp.concatenate([r[:, width:] for r in rows_refs], axis=0).astype(jnp.float32)
    lane = lax.broadcasted_iota(jnp.int32, extra.shape, 1)
    slot = slot_ref[0]
    mine = (lane == slot) | (lane == slot + count)
    gate = jnp.sum(jnp.where(mine, extra, 0.0), axis=1, keepdims=True)
    total = None
    for w in weight_refs:
        g = jnp.dot(rows, w[0, 0], preferred_element_type=jnp.float32)
        u = jnp.dot(rows, w[0, 1], preferred_element_type=jnp.float32)
        hidden = (g / (1.0 + jnp.exp(-g)) * u).astype(jnp.bfloat16)
        part = lax.dot_general(
            hidden, w[0, 2], (((1,), (1,)), ((), ())), preferred_element_type=jnp.float32
        )
        total = part if total is None else total + part
    result = (total * gate).astype(jnp.bfloat16)
    start = 0
    for out in out_refs:
        out[...] = result[start : start + out.shape[0]]
        start += out.shape[0]


def run_expert(slot, row_blocks, shards, width, count):
    blocks = len(row_blocks)
    whole = pl.BlockSpec(memory_space=pltpu.VMEM)
    rows = sum(b.shape[0] for b in row_blocks)
    hidden = sum(s.shape[3] for s in shards)
    return pl.pallas_call(
        functools.partial(expert_kernel, blocks, len(shards), width, count),
        out_shape=[jax.ShapeDtypeStruct((b.shape[0], width), jnp.bfloat16) for b in row_blocks],
        in_specs=[pl.BlockSpec(memory_space=pltpu.SMEM)] + [whole] * (blocks + len(shards)),
        out_specs=[whole] * blocks,
        cost_estimate=pl.CostEstimate(
            flops=6 * rows * width * hidden,
            bytes_accessed=6 * width * hidden + 4 * rows * width,
            transcendentals=rows * hidden,
        ),
    )(slot, *row_blocks, *shards)


def gather_weights(weights, dp_count):
    chips = dp_count // 2
    swap = [(i, i ^ 1) for i in range(dp_count)]
    shards = [weights, lax.ppermute(weights, "dp", swap)]
    for step in range(1, chips):
        turn = [(i, (i + 2 * step) % dp_count) for i in range(dp_count)]
        far = lax.ppermute(weights, "dp", turn)
        shards += [far, lax.ppermute(far, "dp", swap)]
    return shards


def per_device(
    tokens, route_ids, gate_weight, old_owner, new_owner, weights, first_moment, second_moment
):
    count, dp_count = lax.axis_size("expert"), lax.axis_size("dp")
    tok_rows, width = tokens.shape
    labels = jnp.arange(count, dtype=jnp.int32)
    source_slot = jnp.sum(
        jnp.where(new_owner[None, :] == labels[:, None], old_owner[None, :], 0), axis=1
    )
    slot = lax.axis_index("expert").astype(jnp.int32).reshape(1)

    shards = gather_weights(weights, dp_count)

    by_expert = jnp.sum(
        jnp.where(route_ids[:, :, None] == labels[None, None, :], gate_weight[:, :, None], 0.0),
        axis=1,
    )
    by_slot = jnp.sum(
        jnp.where(old_owner[None, None, :] == labels[None, :, None], by_expert[:, None, :], 0.0),
        axis=2,
    )
    high = by_slot.astype(jnp.bfloat16)
    low = (by_slot - high.astype(jnp.float32)).astype(jnp.bfloat16)
    spare = -(-2 * count // LANES) * LANES - 2 * count
    packed = jnp.concatenate([tokens, high, low, jnp.zeros((tok_rows, spare), jnp.bfloat16)], axis=1)

    ahead, behind = ring_pairs(count)
    steps = count // 2
    half = tok_rows // 2
    from_behind, from_ahead = [packed], [packed]
    for step in range(1, steps):
        from_behind.append(lax.ppermute(from_behind[-1], "expert", ahead))
        from_ahead.append(lax.ppermute(from_ahead[-1], "expert", behind))
    far_first = lax.ppermute(from_behind[-1][:half], "expert", ahead)
    far_second = lax.ppermute(from_ahead[-1][half:], "expert", behind)

    moved_weights, moved_first, moved_second = relocate(
        (weights, first_moment, second_moment), old_owner, new_owner, source_slot, dp_count, count
    )

    apply = functools.partial(run_expert, slot, shards=shards, width=width, count=count)
    own, *near = apply([packed] + [b for b in (from_behind[1], from_ahead[1])])
    answers = {1: near}
    for step in range(2, steps):
        answers[step] = apply([from_behind[step], from_ahead[step]])
    top, bottom = apply([far_first, far_second])

    def add(a, b):
        return (a.astype(jnp.float32) + b.astype(jnp.float32)).astype(jnp.bfloat16)

    to_behind = lax.ppermute(top, "expert", behind)
    to_ahead = lax.ppermute(bottom, "expert", ahead)
    for step in range(steps - 1, 0, -1):
        back, front = answers[step]
        if step == steps - 1:
            back = jnp.concatenate([add(back[:half], to_behind), back[half:]], axis=0)
            front = jnp.concatenate([front[:half], add(front[half:], to_ahead)], axis=0)
        else:
            back, front = add(back, to_behind), add(front, to_ahead)
        to_behind = lax.ppermute(back, "expert", behind)
        to_ahead = lax.ppermute(front, "expert", ahead)
    layer_output = (
        own.astype(jnp.float32) + to_behind.astype(jnp.float32) + to_ahead.astype(jnp.float32)
    ).astype(jnp.bfloat16)
    return (layer_output, moved_weights, moved_first, moved_second)


def solution(mesh):
    placed = (
        P(("dp", "expert"), None),
        P(("dp", "expert"), None),
        P(("dp", "expert"), None),
        P(),
        P(),
        P("expert", None, None, "dp"),
        P("expert", None, None, "dp"),
        P("expert", None, None, "dp"),
    )
    return jax.shard_map(
        per_device,
        mesh=mesh,
        in_specs=placed,
        out_specs=(
            P(("dp", "expert"), None),
            P("expert", None, None, "dp"),
            P("expert", None, None, "dp"),
            P("expert", None, None, "dp"),
        ),
        check_vma=False,
    )
```

```python
import functools
import itertools

import jax
import jax.numpy as jnp
from jax import lax
from jax.experimental import pallas as pl
from jax.experimental.pallas import tpu as pltpu
from jax.sharding import PartitionSpec as P


LANES = 128
PAIR_LIMIT = 64


def ring_pairs(count, hops):
    order = list(range(0, count, 2)) + list(range(1, count, 2))[::-1]
    ahead = [(order[i], order[(i + hops) % count]) for i in range(count)]
    return ahead, [(b, a) for a, b in ahead]


def relay_of(source, target, count):
    if source ^ 1 != target:
        return source ^ 1
    beyond = target + 2
    return beyond if beyond < count else target - 2


def swap_slots(pair, dp_count, count, weights, moments):
    low, high = pair
    low_relay, high_relay = relay_of(low, high, count), relay_of(high, low, count)

    def spread(core, edges):
        return [
            (row * count + a, row * count + b) for row in range(core, dp_count, 2) for a, b in edges
        ]

    swap = [(low, high), (high, low)]
    first_hop = spread(1, [(low, low_relay), (high, high_relay)])
    second_hop = spread(1, [(low_relay, high), (high_relay, low)])
    axes = ("dp", "expert")
    direct = lax.ppermute(moments, axes, spread(0, swap) + first_hop)
    moved_weights = lax.ppermute(weights, axes, spread(0, swap) + spread(1, swap))
    relayed = lax.ppermute(direct, axes, second_hop)
    return moved_weights, direct, relayed


def any_permutation(source_slot, weights, moments):
    count = lax.axis_size("expert")

    def move(block):
        rows = block.reshape(count, -1, block.shape[-1])
        spread = lax.all_to_all(rows, "expert", split_axis=0, concat_axis=0, tiled=True)
        ordered = jnp.take(spread, source_slot, axis=0)
        back = lax.all_to_all(ordered, "expert", split_axis=0, concat_axis=0, tiled=True)
        return back.reshape(block.shape)

    moved = move(moments)
    return move(weights), moved, moved


def relocate(weights, moments, old_owner, new_owner, source_slot, dp_count, count):
    packed = jnp.concatenate([m.astype(jnp.bfloat16) for m in moments], axis=0)
    pairs = list(itertools.combinations(range(count), 2))
    if len(pairs) > PAIR_LIMIT:
        return any_permutation(source_slot, weights, packed)
    differs = old_owner != new_owner
    low = jnp.min(jnp.where(differs, old_owner, count))
    high = jnp.max(jnp.where(differs, old_owner, 0))
    number = low * count - low * (low + 1) // 2 + high - low - 1
    branch = jnp.where(jnp.sum(differs.astype(jnp.int32)) == 2, number, len(pairs))
    branches = [
        functools.partial(lambda pair, *p: swap_slots(pair, dp_count, count, *p), pair)
        for pair in pairs
    ] + [lambda *p: any_permutation(source_slot, *p)]
    return lax.switch(branch, branches, weights, packed)


def expert_kernel(blocks, shards, width, count, slot_ref, *refs):
    rows_refs, weight_refs, out_refs = (
        refs[:blocks],
        refs[blocks : blocks + shards],
        refs[blocks + shards :],
    )
    rows = jnp.concatenate([r[:, :width] for r in rows_refs], axis=0)
    extra = jnp.concatenate([r[:, width:] for r in rows_refs], axis=0).astype(jnp.float32)
    lane = lax.broadcasted_iota(jnp.int32, extra.shape, 1)
    slot = slot_ref[0]
    mine = (lane == slot) | (lane == slot + count)
    gate = jnp.sum(jnp.where(mine, extra, 0.0), axis=1, keepdims=True)
    total = None
    for w in weight_refs:
        g = jnp.dot(rows, w[0, 0], preferred_element_type=jnp.float32)
        u = jnp.dot(rows, w[0, 1], preferred_element_type=jnp.float32)
        hidden = (g / (1.0 + jnp.exp(-g)) * u).astype(jnp.bfloat16)
        part = lax.dot_general(
            hidden, w[0, 2], (((1,), (1,)), ((), ())), preferred_element_type=jnp.float32
        )
        total = part if total is None else total + part
    result = total.astype(jnp.bfloat16).astype(jnp.float32) * gate
    start = 0
    for out in out_refs:
        out[...] = result[start : start + out.shape[0]].astype(out.dtype)
        start += out.shape[0]


def run_expert(slot, row_blocks, dtype, shards, width, count):
    blocks = len(row_blocks)
    whole = pl.BlockSpec(memory_space=pltpu.VMEM)
    rows = sum(b.shape[0] for b in row_blocks)
    hidden = sum(s.shape[3] for s in shards)
    return pl.pallas_call(
        functools.partial(expert_kernel, blocks, len(shards), width, count),
        out_shape=[jax.ShapeDtypeStruct((b.shape[0], width), dtype) for b in row_blocks],
        in_specs=[pl.BlockSpec(memory_space=pltpu.SMEM)] + [whole] * (blocks + len(shards)),
        out_specs=[whole] * blocks,
        cost_estimate=pl.CostEstimate(
            flops=6 * rows * width * hidden,
            bytes_accessed=6 * width * hidden + 6 * rows * width,
            transcendentals=rows * hidden,
        ),
    )(slot, *row_blocks, *shards)


def whole(
    tokens, route_ids, gate_weight, old_owner, new_owner, weights, first_moment, second_moment
):
    count, dp_count = lax.axis_size("expert"), lax.axis_size("dp")
    tok_rows, width = tokens.shape
    odd = lax.axis_index("dp") % 2 == 1
    labels = jnp.arange(count, dtype=jnp.int32)
    source_slot = jnp.sum(
        jnp.where(new_owner[None, :] == labels[:, None], old_owner[None, :], 0), axis=1
    )
    slot = lax.axis_index("expert").astype(jnp.int32)

    swap = [(i, i ^ 1) for i in range(dp_count)]
    far = []
    for step in range(1, dp_count // 2):
        turn = [(i, (i + 2 * step) % dp_count) for i in range(dp_count)]
        far.append(lax.ppermute(weights, "dp", turn))
    shards = [weights, lax.ppermute(weights, "dp", swap)]

    by_expert = jnp.sum(
        jnp.where(route_ids[:, :, None] == labels[None, None, :], gate_weight[:, :, None], 0.0),
        axis=1,
    )
    by_slot = jnp.sum(
        jnp.where(old_owner[None, None, :] == labels[None, :, None], by_expert[:, None, :], 0.0),
        axis=2,
    )
    high = by_slot.astype(jnp.bfloat16)
    low = (by_slot - high.astype(jnp.float32)).astype(jnp.bfloat16)
    spare = -(-2 * count // LANES) * LANES - 2 * count
    packed = jnp.concatenate([tokens, high, low, jnp.zeros((tok_rows, spare), jnp.bfloat16)], axis=1)

    ahead, behind = ring_pairs(count, 1)
    ahead_two, behind_two = ring_pairs(count, 2)
    opposite = [
        (row * count + a, row * count + b)
        for row in range(dp_count)
        for a, b in (behind if row % 2 else ahead)
    ]
    back_again = [(b, a) for a, b in opposite]
    steps = count // 2
    from_behind = [packed, lax.ppermute(packed, "expert", ahead)]
    from_ahead = [packed, lax.ppermute(packed, "expert", behind)]
    if steps > 2:
        from_behind.append(lax.ppermute(packed, "expert", ahead_two))
        from_ahead.append(lax.ppermute(packed, "expert", behind_two))

    moved = relocate(
        weights,
        (first_moment, second_moment),
        old_owner,
        new_owner,
        source_slot,
        dp_count,
        count,
    )
    moved, far, from_behind[1:], from_ahead[1:] = lax.optimization_barrier(
        (moved, far, from_behind[1:], from_ahead[1:])
    )
    for shard in far:
        shards += [shard, lax.ppermute(shard, "dp", swap)]
    for _ in range(3, steps):
        from_behind.append(lax.ppermute(from_behind[-1], "expert", ahead))
        from_ahead.append(lax.ppermute(from_ahead[-1], "expert", behind))
    farthest = lax.ppermute(
        jnp.where(odd, from_ahead[-1], from_behind[-1]), ("dp", "expert"), opposite
    )

    apply = functools.partial(
        run_expert, slot.reshape(1), shards=shards, width=width, count=count
    )
    own, *near = apply([packed, from_behind[1], from_ahead[1]], jnp.float32)
    answers = {1: near}
    for step in range(2, steps):
        answers[step] = apply([from_behind[step], from_ahead[step]], jnp.float32)
    (outermost,) = apply([farthest], jnp.bfloat16)

    arrived = lax.ppermute(outermost, ("dp", "expert"), back_again).astype(jnp.float32)
    to_behind, to_ahead = jnp.where(odd, 0.0, arrived), jnp.where(odd, arrived, 0.0)
    for step in range(steps - 1, 0, -1):
        back, front = answers[step]
        back = (back + to_behind).astype(jnp.bfloat16)
        front = (front + to_ahead).astype(jnp.bfloat16)
        to_behind = lax.ppermute(back, "expert", behind).astype(jnp.float32)
        to_ahead = lax.ppermute(front, "expert", ahead).astype(jnp.float32)
    layer_output = (own + to_behind + to_ahead).astype(jnp.bfloat16)

    here = jnp.sum(jnp.where(labels == slot, source_slot, 0)) != slot
    moved_weights, direct, relayed = moved
    new_weights = jnp.where(here, moved_weights, weights)
    new_moments = [
        jnp.where(here, jnp.where(odd, relayed[i], direct[i]).astype(m.dtype), m[0])[None]
        for i, m in enumerate((first_moment, second_moment))
    ]
    return (layer_output, new_weights, *new_moments)


def solution(mesh):
    placed = (
        P(("dp", "expert"), None),
        P(("dp", "expert"), None),
        P(("dp", "expert"), None),
        P(),
        P(),
        P("expert", None, None, "dp"),
        P("expert", None, None, "dp"),
        P("expert", None, None, "dp"),
    )
    return jax.shard_map(
        whole,
        mesh=mesh,
        in_specs=placed,
        out_specs=(
            P(("dp", "expert"), None),
            P("expert", None, None, "dp"),
            P("expert", None, None, "dp"),
            P("expert", None, None, "dp"),
        ),
        check_vma=False,
    )
```

```python
import functools
import itertools

import jax
import jax.numpy as jnp
from jax import lax
from jax.experimental import pallas as pl
from jax.experimental.pallas import tpu as pltpu
from jax.sharding import PartitionSpec as P


LANES = 128
PAIR_LIMIT = 64


def ring_pairs(count):
    order = list(range(0, count, 2)) + list(range(1, count, 2))[::-1]
    ahead = [(order[i], order[(i + 1) % count]) for i in range(count)]
    return ahead, [(b, a) for a, b in ahead]


def relay_of(source, target, count):
    if source ^ 1 != target:
        return source ^ 1
    beyond = target + 2
    return beyond if beyond < count else target - 2


def swap_slots(pair, dp_count, count, weights, moments):
    low, high = pair
    low_relay, high_relay = relay_of(low, high, count), relay_of(high, low, count)

    def spread(core, edges):
        return [
            (row * count + a, row * count + b) for row in range(core, dp_count, 2) for a, b in edges
        ]

    swap = [(low, high), (high, low)]
    first_hop = spread(1, [(low, low_relay), (high, high_relay)])
    second_hop = spread(1, [(low_relay, high), (high_relay, low)])
    axes = ("dp", "expert")
    direct = lax.ppermute(moments, axes, spread(0, swap) + first_hop)
    moved_weights = lax.ppermute(weights, axes, spread(0, swap) + spread(1, swap))
    relayed = lax.ppermute(direct, axes, second_hop)
    return moved_weights, direct, relayed


def any_permutation(source_slot, weights, moments):
    count = lax.axis_size("expert")

    def move(block):
        rows = block.reshape(count, -1, block.shape[-1])
        spread = lax.all_to_all(rows, "expert", split_axis=0, concat_axis=0, tiled=True)
        ordered = jnp.take(spread, source_slot, axis=0)
        back = lax.all_to_all(ordered, "expert", split_axis=0, concat_axis=0, tiled=True)
        return back.reshape(block.shape)

    moved = move(moments)
    return move(weights), moved, moved


def pack_kernel(first_ref, second_ref, out_ref):
    out_ref[0] = first_ref[0].astype(jnp.bfloat16)
    out_ref[1] = second_ref[0].astype(jnp.bfloat16)


def pack_moments(first_moment, second_moment):
    _, parts, rows, lanes = first_moment.shape
    block = (1, 1, rows, lanes)
    return pl.pallas_call(
        pack_kernel,
        grid=(parts,),
        out_shape=jax.ShapeDtypeStruct((2, parts, rows, lanes), jnp.bfloat16),
        in_specs=[pl.BlockSpec(block, lambda i: (0, i, 0, 0))] * 2,
        out_specs=pl.BlockSpec((2, 1, rows, lanes), lambda i: (0, i, 0, 0)),
        cost_estimate=pl.CostEstimate(
            flops=first_moment.size, bytes_accessed=12 * first_moment.size, transcendentals=0
        ),
    )(first_moment, second_moment)


def relocate(weights, packed, ring, finish, old_owner, new_owner, source_slot, dp_count, count):
    pairs = list(itertools.combinations(range(count), 2))
    if len(pairs) > PAIR_LIMIT:
        return any_permutation(source_slot, weights, packed), finish(*ring)
    differs = old_owner != new_owner
    low = jnp.min(jnp.where(differs, old_owner, count))
    high = jnp.max(jnp.where(differs, old_owner, 0))
    number = low * count - low * (low + 1) // 2 + high - low - 1
    branch = jnp.where(jnp.sum(differs.astype(jnp.int32)) == 2, number, len(pairs))

    def moving(pair, weights, packed, ring):
        return swap_slots(pair, dp_count, count, weights, packed), finish(*ring)

    branches = [functools.partial(moving, pair) for pair in pairs] + [
        lambda weights, packed, ring: (any_permutation(source_slot, weights, packed), finish(*ring))
    ]
    return lax.switch(branch, branches, weights, packed, ring)


def expert_kernel(blocks, shards, width, count, slot_ref, *refs):
    rows_refs, weight_refs, out_refs = (
        refs[:blocks],
        refs[blocks : blocks + shards],
        refs[blocks + shards :],
    )
    rows = jnp.concatenate([r[:, :width] for r in rows_refs], axis=0)
    extra = jnp.concatenate([r[:, width:] for r in rows_refs], axis=0).astype(jnp.float32)
    lane = lax.broadcasted_iota(jnp.int32, extra.shape, 1)
    slot = slot_ref[0]
    mine = (lane == slot) | (lane == slot + count)
    gate = jnp.sum(jnp.where(mine, extra, 0.0), axis=1, keepdims=True)
    total = None
    for w in weight_refs:
        g = jnp.dot(rows, w[0, 0], preferred_element_type=jnp.float32)
        u = jnp.dot(rows, w[0, 1], preferred_element_type=jnp.float32)
        hidden = (g / (1.0 + jnp.exp(-g)) * u).astype(jnp.bfloat16)
        part = lax.dot_general(
            hidden, w[0, 2], (((1,), (1,)), ((), ())), preferred_element_type=jnp.float32
        )
        total = part if total is None else total + part
    result = total.astype(jnp.bfloat16).astype(jnp.float32) * gate
    start = 0
    for out in out_refs:
        out[...] = result[start : start + out.shape[0]].astype(out.dtype)
        start += out.shape[0]


def run_expert(slot, row_blocks, dtype, shards, width, count):
    blocks = len(row_blocks)
    whole = pl.BlockSpec(memory_space=pltpu.VMEM)
    rows = sum(b.shape[0] for b in row_blocks)
    hidden = sum(s.shape[3] for s in shards)
    return pl.pallas_call(
        functools.partial(expert_kernel, blocks, len(shards), width, count),
        out_shape=[jax.ShapeDtypeStruct((b.shape[0], width), dtype) for b in row_blocks],
        in_specs=[pl.BlockSpec(memory_space=pltpu.SMEM)] + [whole] * (blocks + len(shards)),
        out_specs=[whole] * blocks,
        cost_estimate=pl.CostEstimate(
            flops=6 * rows * width * hidden,
            bytes_accessed=6 * width * hidden + 6 * rows * width,
            transcendentals=rows * hidden,
        ),
    )(slot, *row_blocks, *shards)


def whole(
    tokens, route_ids, gate_weight, old_owner, new_owner, weights, first_moment, second_moment
):
    count, dp_count = lax.axis_size("expert"), lax.axis_size("dp")
    tok_rows, width = tokens.shape
    odd = lax.axis_index("dp") % 2 == 1
    labels = jnp.arange(count, dtype=jnp.int32)
    source_slot = jnp.sum(
        jnp.where(new_owner[None, :] == labels[:, None], old_owner[None, :], 0), axis=1
    )
    slot = lax.axis_index("expert").astype(jnp.int32)

    swap = [(i, i ^ 1) for i in range(dp_count)]
    far = []
    for step in range(1, dp_count // 2):
        turn = [(i, (i + 2 * step) % dp_count) for i in range(dp_count)]
        far.append(lax.ppermute(weights, "dp", turn))
    by_expert = jnp.sum(
        jnp.where(route_ids[:, :, None] == labels[None, None, :], gate_weight[:, :, None], 0.0),
        axis=1,
    )
    by_slot = jnp.sum(
        jnp.where(old_owner[None, None, :] == labels[None, :, None], by_expert[:, None, :], 0.0),
        axis=2,
    )
    high = by_slot.astype(jnp.bfloat16)
    low = (by_slot - high.astype(jnp.float32)).astype(jnp.bfloat16)
    spare = -(-2 * count // LANES) * LANES - 2 * count
    packed = jnp.concatenate([tokens, high, low, jnp.zeros((tok_rows, spare), jnp.bfloat16)], axis=1)

    ahead, behind = ring_pairs(count)
    opposite = [
        (row * count + a, row * count + b)
        for row in range(dp_count)
        for a, b in (behind if row % 2 else ahead)
    ]
    steps = count // 2
    from_behind, from_ahead = [packed], [packed]
    for _ in range(1, min(3, steps)):
        from_behind.append(lax.ppermute(from_behind[-1], "expert", ahead))
        from_ahead.append(lax.ppermute(from_ahead[-1], "expert", behind))

    def finish(back, front):
        backs, fronts = [], []
        for _ in range(3, steps):
            back = lax.ppermute(back, "expert", ahead)
            front = lax.ppermute(front, "expert", behind)
            backs.append(back)
            fronts.append(front)
        outer = lax.ppermute(jnp.where(odd, front, back), ("dp", "expert"), opposite)
        return backs, fronts, outer

    moments = pack_moments(first_moment, second_moment)
    moved, (backs, fronts, farthest) = relocate(
        weights,
        moments,
        (from_behind[-1], from_ahead[-1]),
        finish,
        old_owner,
        new_owner,
        source_slot,
        dp_count,
        count,
    )
    from_behind += backs
    from_ahead += fronts
    far, moved = lax.optimization_barrier((far, moved))
    near = lax.ppermute(weights, "dp", swap)
    shards = [weights, near]
    for shard in far:
        shard, near = lax.optimization_barrier((shard, near))
        near = lax.ppermute(shard, "dp", swap)
        shards += [shard, near]

    apply = functools.partial(
        run_expert, slot.reshape(1), shards=shards, width=width, count=count
    )
    (outermost,) = apply([farthest], jnp.bfloat16)
    answers = {}
    for step in range(steps - 1, 1, -1):
        answers[step] = apply([from_behind[step], from_ahead[step]], jnp.float32)
    own, *answers[1] = apply([packed, from_behind[1], from_ahead[1]], jnp.float32)

    arrived = lax.ppermute(outermost, ("dp", "expert"), opposite).astype(jnp.float32)
    to_behind, to_ahead = jnp.where(odd, arrived, 0.0), jnp.where(odd, 0.0, arrived)
    for step in range(steps - 1, 0, -1):
        back, front = answers[step]
        back = (back + to_behind).astype(jnp.bfloat16)
        front = (front + to_ahead).astype(jnp.bfloat16)
        to_behind = lax.ppermute(back, "expert", behind).astype(jnp.float32)
        to_ahead = lax.ppermute(front, "expert", ahead).astype(jnp.float32)
    layer_output = (own + to_behind + to_ahead).astype(jnp.bfloat16)

    here = jnp.sum(jnp.where(labels == slot, source_slot, 0)) != slot
    moved_weights, direct, relayed = moved
    new_weights = jnp.where(here, moved_weights, weights)
    new_moments = [
        jnp.where(here, jnp.where(odd, relayed[i], direct[i]).astype(m.dtype), m[0])[None]
        for i, m in enumerate((first_moment, second_moment))
    ]
    return (layer_output, new_weights, *new_moments)


def solution(mesh):
    placed = (
        P(("dp", "expert"), None),
        P(("dp", "expert"), None),
        P(("dp", "expert"), None),
        P(),
        P(),
        P("expert", None, None, "dp"),
        P("expert", None, None, "dp"),
        P("expert", None, None, "dp"),
    )
    return jax.shard_map(
        whole,
        mesh=mesh,
        in_specs=placed,
        out_specs=(
            P(("dp", "expert"), None),
            P("expert", None, None, "dp"),
            P("expert", None, None, "dp"),
            P("expert", None, None, "dp"),
        ),
        check_vma=False,
    )
```

```python
import functools
import itertools

import jax
import jax.numpy as jnp
from jax import lax
from jax.experimental import pallas as pl
from jax.experimental.pallas import tpu as pltpu
from jax.sharding import PartitionSpec as P


LANES = 128
PAIR_LIMIT = 64


def ring_pairs(count):
    order = list(range(0, count, 2)) + list(range(1, count, 2))[::-1]
    ahead = [(order[i], order[(i + 1) % count]) for i in range(count)]
    return ahead, [(b, a) for a, b in ahead]


def relay_of(source, target, count):
    if source ^ 1 != target:
        return source ^ 1
    beyond = target + 2
    return beyond if beyond < count else target - 2


def swap_slots(pair, dp_count, count, weights, moments):
    low, high = pair
    low_relay, high_relay = relay_of(low, high, count), relay_of(high, low, count)

    def spread(core, edges):
        return [
            (row * count + a, row * count + b) for row in range(core, dp_count, 2) for a, b in edges
        ]

    swap = [(low, high), (high, low)]
    first_hop = spread(1, [(low, low_relay), (high, high_relay)])
    second_hop = spread(1, [(low_relay, high), (high_relay, low)])
    axes = ("dp", "expert")
    direct = lax.ppermute(moments, axes, spread(0, swap) + first_hop)
    moved_weights = lax.ppermute(weights, axes, spread(0, swap) + spread(1, swap))
    relayed = lax.ppermute(direct, axes, second_hop)
    return moved_weights, direct, relayed


def any_permutation(source_slot, weights, moments):
    count = lax.axis_size("expert")

    def move(block):
        rows = block.reshape(count, -1, block.shape[-1])
        spread = lax.all_to_all(rows, "expert", split_axis=0, concat_axis=0, tiled=True)
        ordered = jnp.take(spread, source_slot, axis=0)
        back = lax.all_to_all(ordered, "expert", split_axis=0, concat_axis=0, tiled=True)
        return back.reshape(block.shape)

    moved = move(moments)
    return move(weights), moved, moved


def pack_kernel(first_ref, second_ref, out_ref):
    out_ref[0] = first_ref[0].astype(jnp.bfloat16)
    out_ref[1] = second_ref[0].astype(jnp.bfloat16)


def pack_moments(first_moment, second_moment):
    _, parts, rows, lanes = first_moment.shape
    block = (1, 1, rows, lanes)
    return pl.pallas_call(
        pack_kernel,
        grid=(parts,),
        out_shape=jax.ShapeDtypeStruct((2, parts, rows, lanes), jnp.bfloat16),
        in_specs=[pl.BlockSpec(block, lambda i: (0, i, 0, 0))] * 2,
        out_specs=pl.BlockSpec((2, 1, rows, lanes), lambda i: (0, i, 0, 0)),
        cost_estimate=pl.CostEstimate(
            flops=first_moment.size, bytes_accessed=12 * first_moment.size, transcendentals=0
        ),
    )(first_moment, second_moment)


def relocate(weights, packed, fetch, old_owner, new_owner, source_slot, dp_count, count):
    pairs = list(itertools.combinations(range(count), 2))
    if len(pairs) > PAIR_LIMIT:
        return any_permutation(source_slot, weights, packed), fetch(weights)
    pairs.sort(key=lambda pair: pair[::-1])
    differs = old_owner != new_owner
    low = jnp.min(jnp.where(differs, old_owner, count))
    high = jnp.max(jnp.where(differs, old_owner, 0))
    number = lax.shift_right_logical(high * (high - 1), 1) + low
    branch = jnp.where(jnp.sum(differs.astype(jnp.int32)) == 2, number, len(pairs))

    def moving(pair, weights, packed):
        return swap_slots(pair, dp_count, count, weights, packed), fetch(weights)

    branches = [functools.partial(moving, pair) for pair in pairs] + [
        lambda weights, packed: (any_permutation(source_slot, weights, packed), fetch(weights))
    ]
    return lax.switch(branch, branches, weights, packed)


def expert_kernel(blocks, shards, width, count, slot_ref, *refs):
    rows_refs, weight_refs, out_refs = (
        refs[:blocks],
        refs[blocks : blocks + shards],
        refs[blocks + shards :],
    )
    rows = jnp.concatenate([r[:, :width] for r in rows_refs], axis=0)
    extra = jnp.concatenate([r[:, width:] for r in rows_refs], axis=0).astype(jnp.float32)
    lane = lax.broadcasted_iota(jnp.int32, extra.shape, 1)
    slot = slot_ref[0]
    mine = (lane == slot) | (lane == slot + count)
    gate = jnp.sum(jnp.where(mine, extra, 0.0), axis=1, keepdims=True)
    total = None
    for w in weight_refs:
        g = jnp.dot(rows, w[0, 0], preferred_element_type=jnp.float32)
        u = jnp.dot(rows, w[0, 1], preferred_element_type=jnp.float32)
        hidden = (g / (1.0 + jnp.exp(-g)) * u).astype(jnp.bfloat16)
        part = lax.dot_general(
            hidden, w[0, 2], (((1,), (1,)), ((), ())), preferred_element_type=jnp.float32
        )
        total = part if total is None else total + part
    result = total.astype(jnp.bfloat16).astype(jnp.float32) * gate
    start = 0
    for out in out_refs:
        out[...] = result[start : start + out.shape[0]].astype(out.dtype)
        start += out.shape[0]


def run_expert(slot, row_blocks, dtype, shards, width, count):
    blocks = len(row_blocks)
    whole = pl.BlockSpec(memory_space=pltpu.VMEM)
    rows = sum(b.shape[0] for b in row_blocks)
    hidden = sum(s.shape[3] for s in shards)
    return pl.pallas_call(
        functools.partial(expert_kernel, blocks, len(shards), width, count),
        out_shape=[jax.ShapeDtypeStruct((b.shape[0], width), dtype) for b in row_blocks],
        in_specs=[pl.BlockSpec(memory_space=pltpu.SMEM)] + [whole] * (blocks + len(shards)),
        out_specs=[whole] * blocks,
        cost_estimate=pl.CostEstimate(
            flops=6 * rows * width * hidden,
            bytes_accessed=6 * width * hidden + 6 * rows * width,
            transcendentals=rows * hidden,
        ),
    )(slot, *row_blocks, *shards)


def whole(
    tokens, route_ids, gate_weight, old_owner, new_owner, weights, first_moment, second_moment
):
    count, dp_count = lax.axis_size("expert"), lax.axis_size("dp")
    tok_rows, width = tokens.shape
    odd = lax.bitwise_and(lax.axis_index("dp"), 1) == 1
    labels = jnp.arange(count, dtype=jnp.int32)
    source_slot = jnp.sum(
        jnp.where(new_owner[None, :] == labels[:, None], old_owner[None, :], 0), axis=1
    )
    slot = lax.axis_index("expert").astype(jnp.int32)

    def fetch(block):
        shards = []
        for step in range(1, dp_count // 2):
            turn = [(i, (i + 2 * step) % dp_count) for i in range(dp_count)]
            shards.append(lax.ppermute(block, "dp", turn))
        return shards

    by_expert = jnp.sum(
        jnp.where(route_ids[:, :, None] == labels[None, None, :], gate_weight[:, :, None], 0.0),
        axis=1,
    )
    by_slot = jnp.sum(
        jnp.where(old_owner[None, None, :] == labels[None, :, None], by_expert[:, None, :], 0.0),
        axis=2,
    )
    high = by_slot.astype(jnp.bfloat16)
    low = (by_slot - high.astype(jnp.float32)).astype(jnp.bfloat16)
    spare = -(-2 * count // LANES) * LANES - 2 * count
    packed = jnp.concatenate([tokens, high, low, jnp.zeros((tok_rows, spare), jnp.bfloat16)], axis=1)

    ahead, behind = ring_pairs(count)
    opposite = [
        (row * count + a, row * count + b)
        for row in range(dp_count)
        for a, b in (behind if row % 2 else ahead)
    ]
    swap = [(i, i ^ 1) for i in range(dp_count)]
    steps = count // 2
    from_behind, from_ahead = [packed], [packed]

    def hop():
        from_behind.append(lax.ppermute(from_behind[-1], "expert", ahead))
        from_ahead.append(lax.ppermute(from_ahead[-1], "expert", behind))

    hop()
    shards = [weights, lax.ppermute(weights, "dp", swap)]
    moments = pack_moments(first_moment, second_moment)
    moved, far = relocate(
        weights, moments, fetch, old_owner, new_owner, source_slot, dp_count, count
    )
    moved, from_behind[1], from_ahead[1] = lax.optimization_barrier(
        (moved, from_behind[1], from_ahead[1])
    )
    for shard in far:
        shard, shards[-1] = lax.optimization_barrier((shard, shards[-1]))
        shards += [shard, lax.ppermute(shard, "dp", swap)]

    apply = functools.partial(
        run_expert, slot.reshape(1), shards=shards, width=width, count=count
    )
    answers = {}
    for _ in range(2, steps):
        hop()
    for step in range(1, steps):
        blocks = [from_behind[step], from_ahead[step]] + ([packed] if step == 1 else [])
        answers[step] = list(apply(blocks, jnp.float32))
    own = answers[1].pop()
    farthest = lax.ppermute(
        jnp.where(odd, from_ahead[-1], from_behind[-1]), ("dp", "expert"), opposite
    )
    (outermost,) = apply([farthest], jnp.bfloat16)

    arrived = lax.ppermute(outermost, ("dp", "expert"), opposite).astype(jnp.float32)
    to_behind, to_ahead = jnp.where(odd, arrived, 0.0), jnp.where(odd, 0.0, arrived)
    for step in range(steps - 1, 0, -1):
        back, front = answers[step]
        back = (back + to_behind).astype(jnp.bfloat16)
        front = (front + to_ahead).astype(jnp.bfloat16)
        to_behind = lax.ppermute(back, "expert", behind).astype(jnp.float32)
        to_ahead = lax.ppermute(front, "expert", ahead).astype(jnp.float32)
    layer_output = (own + to_behind + to_ahead).astype(jnp.bfloat16)

    here = jnp.sum(jnp.where(labels == slot, source_slot, 0)) != slot
    moved_weights, direct, relayed = moved
    new_weights = jnp.where(here, moved_weights, weights)
    new_moments = [
        jnp.where(here, jnp.where(odd, relayed[i], direct[i]).astype(m.dtype), m[0])[None]
        for i, m in enumerate((first_moment, second_moment))
    ]
    return (layer_output, new_weights, *new_moments)


def solution(mesh):
    placed = (
        P(("dp", "expert"), None),
        P(("dp", "expert"), None),
        P(("dp", "expert"), None),
        P(),
        P(),
        P("expert", None, None, "dp"),
        P("expert", None, None, "dp"),
        P("expert", None, None, "dp"),
    )
    return jax.shard_map(
        whole,
        mesh=mesh,
        in_specs=placed,
        out_specs=(
            P(("dp", "expert"), None),
            P("expert", None, None, "dp"),
            P("expert", None, None, "dp"),
            P("expert", None, None, "dp"),
        ),
        check_vma=False,
    )
```

```python
import functools
import itertools

import jax
import jax.numpy as jnp
from jax import lax
from jax.experimental import pallas as pl
from jax.experimental.pallas import tpu as pltpu
from jax.sharding import PartitionSpec as P


LANES = 128
PAIR_LIMIT = 64
EXPERT_VMEM = 16 << 20
MOVE_VMEM = 16 << 20


def ring_pairs(count):
    order = list(range(0, count, 2)) + list(range(1, count, 2))[::-1]
    ahead = [(order[i], order[(i + 1) % count]) for i in range(count)]
    return ahead, [(b, a) for a, b in ahead]


def relay_of(source, target, count):
    if source ^ 1 != target:
        return source ^ 1
    beyond = target + 2
    return beyond if beyond < count else target - 2


def swap_slots(pair, dp_count, count, weights, moments):
    low, high = pair
    low_relay, high_relay = relay_of(low, high, count), relay_of(high, low, count)

    def spread(core, edges):
        return [
            (row * count + a, row * count + b) for row in range(core, dp_count, 2) for a, b in edges
        ]

    swap = [(low, high), (high, low)]
    first_hop = spread(1, [(low, low_relay), (high, high_relay)])
    second_hop = spread(1, [(low_relay, high), (high_relay, low)])
    axes = ("dp", "expert")
    direct = lax.ppermute(moments, axes, spread(0, swap) + first_hop)
    moved_weights = lax.ppermute(weights, axes, spread(0, swap) + spread(1, swap))
    relayed = lax.ppermute(direct, axes, second_hop)
    return moved_weights, direct, relayed


def any_permutation(source_slot, weights, moments):
    count, lanes = lax.axis_size("expert"), weights.shape[-1]
    rows = jnp.concatenate([b.reshape(count, -1, lanes) for b in (weights, moments)], axis=1)
    spread = lax.all_to_all(rows, "expert", split_axis=0, concat_axis=0, tiled=True)
    ordered = jnp.take(spread, source_slot, axis=0)
    back = lax.all_to_all(ordered, "expert", split_axis=0, concat_axis=0, tiled=True)
    cut = weights.size // (count * lanes)
    moved = back[:, cut:].reshape(moments.shape)
    return back[:, :cut].reshape(weights.shape), moved, moved


def pack_kernel(first_ref, second_ref, out_ref):
    out_ref[0] = first_ref[0].astype(jnp.bfloat16)
    out_ref[1] = second_ref[0].astype(jnp.bfloat16)


def pack_moments(first_moment, second_moment):
    _, parts, rows, lanes = first_moment.shape
    block = (1, 1, rows, lanes)
    return pl.pallas_call(
        pack_kernel,
        grid=(parts,),
        out_shape=jax.ShapeDtypeStruct((2, parts, rows, lanes), jnp.bfloat16),
        in_specs=[pl.BlockSpec(block, lambda i: (0, i, 0, 0))] * 2,
        out_specs=pl.BlockSpec((2, 1, rows, lanes), lambda i: (0, i, 0, 0)),
        cost_estimate=pl.CostEstimate(
            flops=first_moment.size, bytes_accessed=12 * first_moment.size, transcendentals=0
        ),
    )(first_moment, second_moment)


def unpack_kernel(parts, flags, *refs):
    weights, first, second, arrived, direct, relayed = refs[:6]
    out_weights, out_first, out_second = refs[6:9]
    held, wide, narrow, reads, writes = refs[9:]
    here, odd = flags[0] == 1, flags[1] == 1
    owns, outs = (first, second), (out_first, out_second)
    pieces = [(k, i) for k in range(2) for i in range(parts)]
    last = len(pieces)

    def own_read(n):
        k, i = pieces[n]
        return pltpu.make_async_copy(owns[k].at[0, i], wide.at[n], reads.at[n])

    def moved_read(n, source):
        k, i = pieces[n]
        return pltpu.make_async_copy(source.at[k, i], narrow.at[n], reads.at[n])

    def write(n):
        k, i = pieces[n]
        return pltpu.make_async_copy(wide.at[n], outs[k].at[0, i], writes.at[n])

    to_held = pltpu.make_async_copy(weights, held, reads.at[last])
    to_held_moved = pltpu.make_async_copy(arrived, held, reads.at[last])
    from_held = pltpu.make_async_copy(held, out_weights, writes.at[last])

    @pl.when(jnp.logical_not(here))
    def _():
        for n in range(last):
            own_read(n).start()
        to_held.start()
        for n in range(last):
            own_read(n).wait()
            write(n).start()
        to_held.wait()

    @pl.when(here)
    def _():
        @pl.when(odd)
        def _():
            for n in range(last):
                moved_read(n, relayed).start()

        @pl.when(jnp.logical_not(odd))
        def _():
            for n in range(last):
                moved_read(n, direct).start()

        to_held_moved.start()
        for n in range(last):
            moved_read(n, direct).wait()
            wide[n] = narrow[n].astype(jnp.float32)
            write(n).start()
        to_held_moved.wait()

    from_held.start()
    for n in range(last):
        write(n).wait()
    from_held.wait()


def unpack(flags, weights, first, second, arrived, direct, relayed):
    _, parts, rows, lanes = weights.shape
    anywhere = pl.BlockSpec(memory_space=pl.ANY)
    return pl.pallas_call(
        functools.partial(unpack_kernel, parts),
        out_shape=[jax.ShapeDtypeStruct(a.shape, a.dtype) for a in (weights, first, second)],
        in_specs=[pl.BlockSpec(memory_space=pltpu.SMEM)] + [anywhere] * 6,
        out_specs=[anywhere] * 3,
        scratch_shapes=[
            pltpu.VMEM(weights.shape, weights.dtype),
            pltpu.VMEM((2 * parts, rows, lanes), jnp.float32),
            pltpu.VMEM((2 * parts, rows, lanes), jnp.bfloat16),
            pltpu.SemaphoreType.DMA((2 * parts + 1,)),
            pltpu.SemaphoreType.DMA((2 * parts + 1,)),
        ],
        compiler_params=pltpu.CompilerParams(vmem_limit_bytes=MOVE_VMEM),
        cost_estimate=pl.CostEstimate(
            flops=weights.size, bytes_accessed=20 * weights.size, transcendentals=0
        ),
    )(flags, weights, first, second, arrived, direct, relayed)


def relocate(weights, packed, others, meanwhile, old_owner, new_owner, source_slot, dp_count, count):
    pairs = list(itertools.combinations(range(count), 2))
    if len(pairs) > PAIR_LIMIT:
        return any_permutation(source_slot, weights, packed), meanwhile(weights, *others)
    pairs.sort(key=lambda pair: pair[::-1])
    differs = old_owner != new_owner
    low = jnp.min(jnp.where(differs, old_owner, count))
    high = jnp.max(jnp.where(differs, old_owner, 0))
    number = lax.shift_right_logical(high * (high - 1), 1) + low
    branch = jnp.where(jnp.sum(differs.astype(jnp.int32)) == 2, number, len(pairs))

    def moving(pair, weights, packed, others):
        moved = swap_slots(pair, dp_count, count, weights, packed)
        return moved, meanwhile(weights, *others)

    def moving_any(weights, packed, others):
        return any_permutation(source_slot, weights, packed), meanwhile(weights, *others)

    branches = [functools.partial(moving, pair) for pair in pairs] + [moving_any]
    return lax.switch(branch, branches, weights, packed, others)


def expert_kernel(blocks, shards, tok_rows, slot_ref, *refs):
    rows_refs, far_refs, out_refs = (
        refs[:blocks],
        refs[blocks : blocks + shards],
        refs[blocks + shards : -3],
    )
    held, total, arrivals = refs[-3:]

    def fetch(i, source):
        return pltpu.make_async_copy(source.at[0], held.at[i], arrivals.at[i])

    for i, ref in enumerate(far_refs):
        fetch(i, ref).start()
    rows = jnp.concatenate([r[:tok_rows] for r in rows_refs], axis=0)
    slot = slot_ref[0]
    offset = -(-tok_rows // LANES) * LANES
    gates = []
    for r in rows_refs:
        table = r[tok_rows:].astype(jnp.float32)
        column = (table[:, :offset] + table[:, offset : 2 * offset]).T
        mine = lax.broadcasted_iota(jnp.int32, column.shape, 1) == slot
        column = jnp.sum(jnp.where(mine, column, 0.0), axis=1, keepdims=True)
        gates.append(column[:tok_rows])
    gate = jnp.concatenate(gates, axis=0)
    total[...] = jnp.zeros_like(total)

    @pl.loop(0, shards)
    def _(i):
        fetch(i, far_refs[0]).wait()
        g = jnp.dot(rows, held[i, 0], preferred_element_type=jnp.float32)
        u = jnp.dot(rows, held[i, 1], preferred_element_type=jnp.float32)
        hidden = (g / (1.0 + jnp.exp(-g)) * u).astype(jnp.bfloat16)
        total[...] += lax.dot_general(
            hidden, held[i, 2], (((1,), (1,)), ((), ())), preferred_element_type=jnp.float32
        )

    result = total[...].astype(jnp.bfloat16).astype(jnp.float32) * gate
    start = 0
    for out in out_refs:
        out[...] = result[start : start + out.shape[0]].astype(out.dtype)
        start += out.shape[0]


def run_expert(slot, row_blocks, dtype, pieces, shards, tok_rows):
    blocks = len(row_blocks)
    whole = pl.BlockSpec(memory_space=pltpu.VMEM)
    _, _, width, hidden = shards[0].shape
    rows, hidden = blocks * tok_rows, hidden * len(shards)
    piece = jax.ShapeDtypeStruct((tok_rows // pieces, width), dtype)
    return pl.pallas_call(
        functools.partial(expert_kernel, blocks, len(shards), tok_rows),
        out_shape=[piece] * (pieces * blocks),
        in_specs=[pl.BlockSpec(memory_space=pltpu.SMEM)]
        + [whole] * blocks
        + [pl.BlockSpec(memory_space=pl.ANY)] * len(shards),
        out_specs=[whole] * (pieces * blocks),
        scratch_shapes=[
            pltpu.VMEM((len(shards),) + shards[0].shape[1:], shards[0].dtype),
            pltpu.VMEM((rows, width), jnp.float32),
            pltpu.SemaphoreType.DMA((len(shards),)),
        ],
        compiler_params=pltpu.CompilerParams(vmem_limit_bytes=EXPERT_VMEM),
        cost_estimate=pl.CostEstimate(
            flops=6 * rows * width * hidden,
            bytes_accessed=6 * width * hidden + 6 * rows * width,
            transcendentals=rows * hidden,
        ),
    )(slot, *row_blocks, *shards)


def whole(
    tokens, route_ids, gate_weight, old_owner, new_owner, weights, first_moment, second_moment
):
    count, dp_count = lax.axis_size("expert"), lax.axis_size("dp")
    tok_rows, width = tokens.shape
    odd = lax.bitwise_and(lax.axis_index("dp"), 1) == 1
    labels = jnp.arange(count, dtype=jnp.int32)
    source_slot = jnp.sum(
        jnp.where(new_owner[None, :] == labels[:, None], old_owner[None, :], 0), axis=1
    )
    slot = lax.axis_index("expert").astype(jnp.int32)

    by_expert = jnp.sum(
        jnp.where(route_ids[:, :, None] == labels[None, None, :], gate_weight[:, :, None], 0.0),
        axis=1,
    )
    by_slot = jnp.sum(
        jnp.where(old_owner[None, None, :] == labels[:, None, None], by_expert[None, :, :], 0.0),
        axis=2,
    )
    high = by_slot.astype(jnp.bfloat16)
    low = (by_slot - high.astype(jnp.float32)).astype(jnp.bfloat16)
    offset = -(-tok_rows // LANES) * LANES
    spare = -count % 8
    high = jnp.pad(high, ((0, spare), (0, offset - tok_rows)))
    low = jnp.pad(low, ((0, spare), (0, width - offset - tok_rows)))
    packed = jnp.concatenate([tokens, jnp.concatenate([high, low], axis=1)], axis=0)

    ahead, behind = ring_pairs(count)
    opposite = [
        (row * count + a, row * count + b)
        for row in range(dp_count)
        for a, b in (behind if row % 2 else ahead)
    ]
    swap = [(i, i ^ 1) for i in range(dp_count)]
    steps = count // 2

    def hop(back, front):
        return lax.ppermute(back, "expert", ahead), lax.ppermute(front, "expert", behind)

    def run(shards, blocks, dtype=jnp.float32, pieces=2):
        return list(run_expert(slot.reshape(1), blocks, dtype, pieces, shards, tok_rows))

    hops = {1: hop(packed, packed)}
    moments = pack_moments(first_moment, second_moment)

    def meanwhile(weights, back, front):
        second = hop(back, front) if steps > 2 else ()
        shards = [weights, lax.ppermute(weights, "dp", swap)]
        for step in range(1, dp_count // 2):
            turn = [(i, (i + 2 * step) % dp_count) for i in range(dp_count)]
            far = lax.ppermute(weights, "dp", turn)
            far, shards[-1] = lax.optimization_barrier((far, shards[-1]))
            shards += [far, lax.ppermute(far, "dp", swap)]
        return second, shards[1:]

    moved, (second, shards) = relocate(
        weights,
        moments,
        hops[1],
        meanwhile,
        old_owner,
        new_owner,
        source_slot,
        dp_count,
        count,
    )
    moved = lax.optimization_barrier(moved)
    shards = [weights, *shards]
    if second:
        hops[2] = second
    for step in range(3, steps):
        hops[step] = hop(*hops[step - 1])
    answers = {1: run(shards, [packed, *hops[1]])}
    own, answers[1] = answers[1][:2], answers[1][2:]
    for step in range(2, steps):
        answers[step] = run(shards, list(hops[step]))
    farthest = lax.ppermute(
        jnp.where(odd, *hops[steps - 1][::-1]), ("dp", "expert"), opposite
    )
    (outermost,) = run(shards, [farthest], jnp.bfloat16, 1)
    arrived = lax.ppermute(outermost, ("dp", "expert"), opposite).astype(jnp.float32)

    outputs = []
    for half in range(2):
        part = arrived[half * tok_rows // 2 : (half + 1) * tok_rows // 2]
        to_behind, to_ahead = jnp.where(odd, part, 0.0), jnp.where(odd, 0.0, part)
        for step in range(steps - 1, 0, -1):
            back = (answers[step][half] + to_behind).astype(jnp.bfloat16)
            front = (answers[step][2 + half] + to_ahead).astype(jnp.bfloat16)
            to_behind = lax.ppermute(back, "expert", behind).astype(jnp.float32)
            to_ahead = lax.ppermute(front, "expert", ahead).astype(jnp.float32)
        outputs.append((own[half] + to_behind + to_ahead).astype(jnp.bfloat16))
    layer_output = jnp.concatenate(outputs, axis=0)

    here = jnp.sum(jnp.where(labels == slot, source_slot, 0)) != slot
    flags = jnp.stack([here, odd]).astype(jnp.int32)
    replaced = unpack(flags, weights, first_moment, second_moment, *moved)
    return (layer_output, *replaced)


def solution(mesh):
    placed = (
        P(("dp", "expert"), None),
        P(("dp", "expert"), None),
        P(("dp", "expert"), None),
        P(),
        P(),
        P("expert", None, None, "dp"),
        P("expert", None, None, "dp"),
        P("expert", None, None, "dp"),
    )
    return jax.shard_map(
        whole,
        mesh=mesh,
        in_specs=placed,
        out_specs=(
            P(("dp", "expert"), None),
            P("expert", None, None, "dp"),
            P("expert", None, None, "dp"),
            P("expert", None, None, "dp"),
        ),
        check_vma=False,
    )
```

```python
import functools
import itertools

import jax
import jax.numpy as jnp
from jax import lax
from jax.experimental import pallas as pl
from jax.experimental.pallas import tpu as pltpu
from jax.sharding import PartitionSpec as P


LANES = 128
PAIR_LIMIT = 64
EXPERT_VMEM = 16 << 20
MOVE_VMEM = 16 << 20


def ring_pairs(count):
    order = list(range(0, count, 2)) + list(range(1, count, 2))[::-1]
    ahead = [(order[i], order[(i + 1) % count]) for i in range(count)]
    return ahead, [(b, a) for a, b in ahead]


def relay_of(source, target, count):
    if source ^ 1 != target:
        return source ^ 1
    beyond = target + 2
    return beyond if beyond < count else target - 2


def swap_slots(pair, dp_count, count, weights, moments):
    low, high = pair
    low_relay, high_relay = relay_of(low, high, count), relay_of(high, low, count)

    def spread(core, edges):
        return [
            (row * count + a, row * count + b) for row in range(core, dp_count, 2) for a, b in edges
        ]

    swap = [(low, high), (high, low)]
    first_hop = spread(1, [(low, low_relay), (high, high_relay)])
    second_hop = spread(1, [(low_relay, high), (high_relay, low)])
    axes = ("dp", "expert")
    direct = lax.ppermute(moments, axes, spread(0, swap) + first_hop)
    moved_weights = lax.ppermute(weights, axes, spread(0, swap) + spread(1, swap))
    relayed = lax.ppermute(direct, axes, second_hop)
    return moved_weights, direct, relayed


def any_permutation(source_slot, weights, moments):
    count, lanes = lax.axis_size("expert"), weights.shape[-1]
    rows = jnp.concatenate([b.reshape(count, -1, lanes) for b in (weights, moments)], axis=1)
    spread = lax.all_to_all(rows, "expert", split_axis=0, concat_axis=0, tiled=True)
    ordered = jnp.take(spread, source_slot, axis=0)
    back = lax.all_to_all(ordered, "expert", split_axis=0, concat_axis=0, tiled=True)
    cut = weights.size // (count * lanes)
    moved = back[:, cut:].reshape(moments.shape)
    return back[:, :cut].reshape(weights.shape), moved, moved


def pack_kernel(first_ref, second_ref, out_ref):
    out_ref[0] = first_ref[0].astype(jnp.bfloat16)
    out_ref[1] = second_ref[0].astype(jnp.bfloat16)


def pack_moments(first_moment, second_moment):
    _, parts, rows, lanes = first_moment.shape
    block = (1, 1, rows, lanes)
    return pl.pallas_call(
        pack_kernel,
        grid=(parts,),
        out_shape=jax.ShapeDtypeStruct((2, parts, rows, lanes), jnp.bfloat16),
        in_specs=[pl.BlockSpec(block, lambda i: (0, i, 0, 0))] * 2,
        out_specs=pl.BlockSpec((2, 1, rows, lanes), lambda i: (0, i, 0, 0)),
        cost_estimate=pl.CostEstimate(
            flops=first_moment.size, bytes_accessed=12 * first_moment.size, transcendentals=0
        ),
    )(first_moment, second_moment)


def unpack_kernel(parts, flags, *refs):
    weights, first, second, arrived, direct, relayed = refs[:6]
    out_weights, out_first, out_second = refs[6:9]
    held, wide, narrow, reads, writes = refs[9:]
    here, odd = flags[0] == 1, flags[1] == 1
    owns, outs = (first, second), (out_first, out_second)
    pieces = [(k, i) for k in range(2) for i in range(parts)]
    last = len(pieces)

    def own_read(n):
        k, i = pieces[n]
        return pltpu.make_async_copy(owns[k].at[0, i], wide.at[n], reads.at[n])

    def moved_read(n, source):
        k, i = pieces[n]
        return pltpu.make_async_copy(source.at[k, i], narrow.at[n], reads.at[n])

    def write(n):
        k, i = pieces[n]
        return pltpu.make_async_copy(wide.at[n], outs[k].at[0, i], writes.at[n])

    to_held = pltpu.make_async_copy(weights, held, reads.at[last])
    to_held_moved = pltpu.make_async_copy(arrived, held, reads.at[last])
    from_held = pltpu.make_async_copy(held, out_weights, writes.at[last])

    @pl.when(jnp.logical_not(here))
    def _():
        for n in range(last):
            own_read(n).start()
        to_held.start()
        for n in range(last):
            own_read(n).wait()
            write(n).start()
        to_held.wait()

    @pl.when(here)
    def _():
        @pl.when(odd)
        def _():
            for n in range(last):
                moved_read(n, relayed).start()

        @pl.when(jnp.logical_not(odd))
        def _():
            for n in range(last):
                moved_read(n, direct).start()

        to_held_moved.start()
        for n in range(last):
            moved_read(n, direct).wait()
            wide[n] = narrow[n].astype(jnp.float32)
            write(n).start()
        to_held_moved.wait()

    from_held.start()
    for n in range(last):
        write(n).wait()
    from_held.wait()


def unpack(flags, weights, first, second, arrived, direct, relayed):
    _, parts, rows, lanes = weights.shape
    anywhere = pl.BlockSpec(memory_space=pl.ANY)
    return pl.pallas_call(
        functools.partial(unpack_kernel, parts),
        out_shape=[jax.ShapeDtypeStruct(a.shape, a.dtype) for a in (weights, first, second)],
        in_specs=[pl.BlockSpec(memory_space=pltpu.SMEM)] + [anywhere] * 6,
        out_specs=[anywhere] * 3,
        scratch_shapes=[
            pltpu.VMEM(weights.shape, weights.dtype),
            pltpu.VMEM((2 * parts, rows, lanes), jnp.float32),
            pltpu.VMEM((2 * parts, rows, lanes), jnp.bfloat16),
            pltpu.SemaphoreType.DMA((2 * parts + 1,)),
            pltpu.SemaphoreType.DMA((2 * parts + 1,)),
        ],
        compiler_params=pltpu.CompilerParams(vmem_limit_bytes=MOVE_VMEM),
        cost_estimate=pl.CostEstimate(
            flops=weights.size, bytes_accessed=20 * weights.size, transcendentals=0
        ),
    )(flags, weights, first, second, arrived, direct, relayed)


def relocate(weights, packed, others, meanwhile, old_owner, new_owner, source_slot, dp_count, count):
    pairs = list(itertools.combinations(range(count), 2))
    if len(pairs) > PAIR_LIMIT:
        return any_permutation(source_slot, weights, packed), meanwhile(weights, *others)
    pairs.sort(key=lambda pair: pair[::-1])
    differs = old_owner != new_owner
    low = jnp.min(jnp.where(differs, old_owner, count))
    high = jnp.max(jnp.where(differs, old_owner, 0))
    number = lax.shift_right_logical(high * (high - 1), 1) + low
    branch = jnp.where(jnp.sum(differs.astype(jnp.int32)) == 2, number, len(pairs))

    def moving(pair, weights, packed, others):
        moved = swap_slots(pair, dp_count, count, weights, packed)
        return moved, meanwhile(weights, *others)

    def moving_any(weights, packed, others):
        return any_permutation(source_slot, weights, packed), meanwhile(weights, *others)

    branches = [functools.partial(moving, pair) for pair in pairs] + [moving_any]
    return lax.switch(branch, branches, weights, packed, others)


def expert_kernel(blocks, shards, tok_rows, slot_ref, *refs):
    rows_refs, far_refs, out_refs = (
        refs[:blocks],
        refs[blocks : blocks + shards],
        refs[blocks + shards : -3],
    )
    held, total, arrivals = refs[-3:]

    def fetch(i, source):
        return pltpu.make_async_copy(source.at[0], held.at[i], arrivals.at[i])

    for i, ref in enumerate(far_refs):
        fetch(i, ref).start()
    rows = jnp.concatenate([r[:tok_rows] for r in rows_refs], axis=0)
    slot = slot_ref[0]
    offset = -(-tok_rows // LANES) * LANES
    gates = []
    for r in rows_refs:
        table = r[tok_rows:].astype(jnp.float32)
        column = (table[:, :offset] + table[:, offset : 2 * offset]).T
        mine = lax.broadcasted_iota(jnp.int32, column.shape, 1) == slot
        column = jnp.sum(jnp.where(mine, column, 0.0), axis=1, keepdims=True)
        gates.append(column[:tok_rows])
    gate = jnp.concatenate(gates, axis=0)
    total[...] = jnp.zeros_like(total)

    @pl.loop(0, shards)
    def _(i):
        fetch(i, far_refs[0]).wait()
        g = jnp.dot(rows, held[i, 0], preferred_element_type=jnp.float32)
        u = jnp.dot(rows, held[i, 1], preferred_element_type=jnp.float32)
        hidden = (g / (1.0 + jnp.exp(-g)) * u).astype(jnp.bfloat16)
        total[...] += lax.dot_general(
            hidden, held[i, 2], (((1,), (1,)), ((), ())), preferred_element_type=jnp.float32
        )

    result = total[...].astype(jnp.bfloat16).astype(jnp.float32) * gate
    start = 0
    for out in out_refs:
        out[...] = result[start : start + out.shape[0]].astype(out.dtype)
        start += out.shape[0]


def run_expert(slot, row_blocks, dtype, pieces, shards, tok_rows):
    blocks = len(row_blocks)
    whole = pl.BlockSpec(memory_space=pltpu.VMEM)
    _, _, width, hidden = shards[0].shape
    rows, hidden = blocks * tok_rows, hidden * len(shards)
    piece = jax.ShapeDtypeStruct((tok_rows // pieces, width), dtype)
    return pl.pallas_call(
        functools.partial(expert_kernel, blocks, len(shards), tok_rows),
        out_shape=[piece] * (pieces * blocks),
        in_specs=[pl.BlockSpec(memory_space=pltpu.SMEM)]
        + [whole] * blocks
        + [pl.BlockSpec(memory_space=pl.ANY)] * len(shards),
        out_specs=[whole] * (pieces * blocks),
        scratch_shapes=[
            pltpu.VMEM((len(shards),) + shards[0].shape[1:], shards[0].dtype),
            pltpu.VMEM((rows, width), jnp.float32),
            pltpu.SemaphoreType.DMA((len(shards),)),
        ],
        compiler_params=pltpu.CompilerParams(vmem_limit_bytes=EXPERT_VMEM),
        cost_estimate=pl.CostEstimate(
            flops=6 * rows * width * hidden,
            bytes_accessed=6 * width * hidden + 6 * rows * width,
            transcendentals=rows * hidden,
        ),
    )(slot, *row_blocks, *shards)


def whole(
    tokens, route_ids, gate_weight, old_owner, new_owner, weights, first_moment, second_moment
):
    count, dp_count = lax.axis_size("expert"), lax.axis_size("dp")
    tok_rows, width = tokens.shape
    odd = lax.bitwise_and(lax.axis_index("dp"), 1) == 1
    labels = jnp.arange(count, dtype=jnp.int32)
    source_slot = jnp.sum(
        jnp.where(new_owner[None, :] == labels[:, None], old_owner[None, :], 0), axis=1
    )
    slot = lax.axis_index("expert").astype(jnp.int32)

    by_expert = jnp.sum(
        jnp.where(route_ids[:, :, None] == labels[None, None, :], gate_weight[:, :, None], 0.0),
        axis=1,
    )
    by_slot = jnp.sum(
        jnp.where(old_owner[None, None, :] == labels[:, None, None], by_expert[None, :, :], 0.0),
        axis=2,
    )
    high = by_slot.astype(jnp.bfloat16)
    low = (by_slot - high.astype(jnp.float32)).astype(jnp.bfloat16)
    offset = -(-tok_rows // LANES) * LANES
    spare = -count % 8
    high = jnp.pad(high, ((0, spare), (0, offset - tok_rows)))
    low = jnp.pad(low, ((0, spare), (0, width - offset - tok_rows)))
    packed = jnp.concatenate([tokens, jnp.concatenate([high, low], axis=1)], axis=0)

    ahead, behind = ring_pairs(count)
    opposite = [
        (row * count + a, row * count + b)
        for row in range(dp_count)
        for a, b in (behind if row % 2 else ahead)
    ]
    swap = [(i, i ^ 1) for i in range(dp_count)]
    steps = count // 2

    def hop(back, front):
        return lax.ppermute(back, "expert", ahead), lax.ppermute(front, "expert", behind)

    def run(shards, blocks, dtype=jnp.float32, pieces=2):
        return list(run_expert(slot.reshape(1), blocks, dtype, pieces, shards, tok_rows))

    hops = {1: hop(packed, packed)}
    moments = pack_moments(first_moment, second_moment)

    def meanwhile(weights, back, front):
        second = hop(back, front) if steps > 2 else ()
        shards = [weights, lax.ppermute(weights, "dp", swap)]
        for step in range(1, dp_count // 2):
            turn = [(i, (i + 2 * step) % dp_count) for i in range(dp_count)]
            far = lax.ppermute(weights, "dp", turn)
            far, shards[-1] = lax.optimization_barrier((far, shards[-1]))
            shards += [far, lax.ppermute(far, "dp", swap)]
        return second, shards[1:]

    moved, (second, shards) = relocate(
        weights,
        moments,
        hops[1],
        meanwhile,
        old_owner,
        new_owner,
        source_slot,
        dp_count,
        count,
    )
    moved = lax.optimization_barrier(moved)
    shards = [weights, *shards]
    if second:
        hops[2] = second
    for step in range(3, steps):
        hops[step] = hop(*hops[step - 1])
    answers = {1: run(shards, [packed, *hops[1]])}
    own, answers[1] = answers[1][:2], answers[1][2:]
    for step in range(2, steps):
        answers[step] = run(shards, list(hops[step]))
    farthest = lax.ppermute(
        jnp.where(odd, *hops[steps - 1][::-1]), ("dp", "expert"), opposite
    )
    (outermost,) = run(shards, [farthest], jnp.bfloat16, 1)
    arrived = lax.ppermute(outermost, ("dp", "expert"), opposite).astype(jnp.float32)

    outputs = []
    for half in range(2):
        part = arrived[half * tok_rows // 2 : (half + 1) * tok_rows // 2]
        to_behind, to_ahead = jnp.where(odd, part, 0.0), jnp.where(odd, 0.0, part)
        for step in range(steps - 1, 0, -1):
            back = (answers[step][half] + to_behind).astype(jnp.bfloat16)
            front = (answers[step][2 + half] + to_ahead).astype(jnp.bfloat16)
            to_behind = lax.ppermute(back, "expert", behind).astype(jnp.float32)
            to_ahead = lax.ppermute(front, "expert", ahead).astype(jnp.float32)
        outputs.append((to_behind, to_ahead, own[half]))
    back, front, kept = (jnp.concatenate(parts, axis=0) for parts in zip(*outputs))
    layer_output = (kept + back + front).astype(jnp.bfloat16)

    here = jnp.sum(jnp.where(labels == slot, source_slot, 0)) != slot
    flags = jnp.stack([here, odd]).astype(jnp.int32)
    replaced = unpack(flags, weights, first_moment, second_moment, *moved)
    return (layer_output, *replaced)


def solution(mesh):
    placed = (
        P(("dp", "expert"), None),
        P(("dp", "expert"), None),
        P(("dp", "expert"), None),
        P(),
        P(),
        P("expert", None, None, "dp"),
        P("expert", None, None, "dp"),
        P("expert", None, None, "dp"),
    )
    return jax.shard_map(
        whole,
        mesh=mesh,
        in_specs=placed,
        out_specs=(
            P(("dp", "expert"), None),
            P("expert", None, None, "dp"),
            P("expert", None, None, "dp"),
            P("expert", None, None, "dp"),
        ),
        check_vma=False,
    )
```
